256 devices in a mesh: row: 8 (over x, y_lo), col: 32 (over z, y_hi, core).
Axes of the slice: x: 4, y: 4 (y_hi: 2, y_lo: 2; y = y_hi * 2 + y_lo), z: 8, core: 2. Of those that a mesh axis runs over, the one named last changes fastest.
Arguments:
- covariance: float32 [12288, 12288], P('row', 'col'), may hold values from -25 to 25, as said below
- process_noise: float32 [12288, 12288], P('row', 'col'), may hold values from -3 to 3, as said below
- wind_heading: int32 [12288], replicated, may hold values from 0 to 7
- wind_speed: int32 [12288], replicated, may hold values from 0 to 7
- mixing_index: int32 [12288], replicated, may hold values from 0 to 7
Outputs:
- forecast: float32 [12288, 12288], P('row', 'col')
The draws below stay inside these ranges and needn't reach their ends.
Inputs may be any that keep to these rules, and one draw needn't show every extreme that they name: `covariance`: symmetric. `process_noise`: symmetric.
All inputs are finite; a program needn't handle non-finite values.
Results may differ from the reference program's by a relative error of at most 0.00002.
Values sent between devices are 32-bit elements; how exact they have to be, the bound alone decides.
No kernel may reach another device: no remote copies, remote signals or barrier semaphores. Data moves between devices by JAX's collectives and lax.ppermute only.
A program may use at most 64 MiB of HBM per device.

```python
import jax
import jax.numpy as jnp
from jax import lax

GY = 96
STEPS = 4
CELLS = 12288


def symmetric_draw(key, diag_add, factor):
    key_base = jax.random.fold_in(key, 0)
    base = jnp.clip(jax.random.normal(key_base, (CELLS, CELLS), jnp.float32), -4.0, 4.0)
    summed = factor * (base + base.T)
    places = jnp.arange(CELLS, dtype=jnp.int32)
    summed = summed.at[places, places].add(diag_add)
    return summed


def draw_covariance(key, part):
    return symmetric_draw(jax.random.fold_in(key, 11), 2.0, 0.5)


def draw_process_noise(key, part):
    key_noise = jax.random.fold_in(key, 23)
    key_base = jax.random.fold_in(key_noise, 1)
    base = jnp.clip(jax.random.normal(key_base, (CELLS, CELLS), jnp.float32), -4.0, 4.0)
    summed = 0.25 * (base + base.T)
    places = jnp.arange(CELLS, dtype=jnp.int32)
    return summed.at[places, places].add(0.5)


def place_ends(entries, rng, smallest, largest):
    longest = entries.shape.index(max(entries.shape))
    spots = []
    for shift in (0, 1):
        where = [jax.random.randint(jax.random.fold_in(rng, axis), (), 0, length) for axis, length in enumerate(entries.shape)]
        where[longest] = (where[longest] + shift) % entries.shape[longest]
        spots.append(tuple(where))
    return entries.at[spots[0]].set(smallest).at[spots[1]].set(largest)


def setup_inputs(seed: int = 0) -> dict:
    splits = jax.random.split(jax.random.key(seed), 6)
    return {
        "covariance": draw_covariance(jax.random.fold_in(splits[5], 71), 0),
        "process_noise": draw_process_noise(jax.random.fold_in(splits[5], 71), 0),
        "wind_heading": place_ends(jax.random.randint(splits[2], (CELLS,), 0, 8), jax.random.fold_in(splits[2], 1), 0, 7).astype(jnp.int32),
        "wind_speed": place_ends(jax.random.randint(splits[3], (CELLS,), 0, 8), jax.random.fold_in(splits[3], 1), 0, 7).astype(jnp.int32),
        "mixing_index": place_ends(jax.random.randint(splits[4], (CELLS,), 0, 8), jax.random.fold_in(splits[4], 1), 0, 7).astype(jnp.int32),
    }


def coefficients(wind_heading, wind_speed, mixing_index, cross_cells, margin):
    heading = (jnp.pi / 4.0) * wind_heading.astype(jnp.float32)
    wind_rate = 0.1 + 0.075 * wind_speed.astype(jnp.float32)
    mixing = 0.02 + 0.02 * mixing_index.astype(jnp.float32)
    east_flow = wind_rate * jnp.cos(heading)
    north_flow = wind_rate * jnp.sin(heading)
    from_west = jnp.maximum(east_flow, 0.0) + mixing
    from_east = jnp.maximum(-east_flow, 0.0) + mixing
    from_south = jnp.maximum(north_flow, 0.0) + mixing
    from_north = jnp.maximum(-north_flow, 0.0) + mixing
    cell_count = wind_heading.shape[0]
    cell_index = jnp.arange(cell_count, dtype=jnp.int32)
    across_pos = cell_index % cross_cells
    along_pos = cell_index // cross_cells
    last_row = cell_count // cross_cells - 1
    stacked = jnp.stack([
        1.0 - from_west - from_east,
        jnp.where(along_pos > 0, from_west, 0.0),
        jnp.where(along_pos < last_row, from_east, 0.0),
        1.0 - from_south - from_north,
        jnp.where(across_pos > 0, from_south, 0.0),
        jnp.where(across_pos < cross_cells - 1, from_north, 0.0),
    ])
    return jnp.pad(stacked, ((0, 0), (margin, margin)))


def advance(extended, weights, cross_cells, which_dim):
    extent = extended.shape[which_dim]
    middle = lax.slice_in_dim(extended, cross_cells, extent - cross_cells, axis=which_dim)
    lower_side = lax.slice_in_dim(extended, 0, extent - 2 * cross_cells, axis=which_dim)
    upper_side = lax.slice_in_dim(extended, 2 * cross_cells, extent, axis=which_dim)
    along_x = weights[0] * middle + weights[1] * lower_side + weights[2] * upper_side
    length = along_x.shape[which_dim]
    zero_line = jnp.zeros_like(lax.slice_in_dim(along_x, 0, 1, axis=which_dim))
    prior_y = jnp.concatenate([zero_line, lax.slice_in_dim(along_x, 0, length - 1, axis=which_dim)], axis=which_dim)
    next_y = jnp.concatenate([lax.slice_in_dim(along_x, 1, length, axis=which_dim), zero_line], axis=which_dim)
    return weights[3] * along_x + weights[4] * prior_y + weights[5] * next_y


def propagate_rows(block, weight_table):
    field = block
    for repeat in range(STEPS):
        field = advance(jnp.pad(field, ((0, 0), (GY, GY))), weight_table[:, None, :], GY, 1)
    return field


def reference(covariance, process_noise, wind_heading, wind_speed, mixing_index):
    weight_table = coefficients(wind_heading, wind_speed, mixing_index, GY, 0)
    height = CELLS // 32

    def sweep_rows(matrix):
        def one_block(part_rows):
            return propagate_rows(part_rows, weight_table)
        return lax.map(one_block, matrix.reshape(32, height, CELLS)).reshape(CELLS, CELLS)

    advected = sweep_rows(covariance.T).T
    return sweep_rows(advected) + process_noise
```

```python
import jax
import jax.numpy as jnp
from jax import lax
from jax.sharding import PartitionSpec as P

GY = 96
STEPS = 4
HALO = STEPS * GY


def window_weights(codes, start, length, cell_count):
    position = start + jnp.arange(length, dtype=jnp.int32)
    heading_code, speed_code, mixing_code = [
        lax.dynamic_slice_in_dim(jnp.pad(code, (HALO, HALO)), start + HALO, length, 0)
        for code in codes
    ]
    heading = jnp.pi / 4.0 * heading_code.astype(jnp.float32)
    wind_rate = 0.1 + 0.075 * speed_code.astype(jnp.float32)
    mixing = 0.02 + 0.02 * mixing_code.astype(jnp.float32)
    east_flow = wind_rate * jnp.cos(heading)
    north_flow = wind_rate * jnp.sin(heading)
    from_west = jnp.maximum(east_flow, 0.0) + mixing
    from_east = jnp.maximum(-east_flow, 0.0) + mixing
    from_south = jnp.maximum(north_flow, 0.0) + mixing
    from_north = jnp.maximum(-north_flow, 0.0) + mixing
    inside = (position >= 0) & (position < cell_count)
    across_pos = (position + HALO) % GY
    stacked = [
        1.0 - from_west - from_east,
        jnp.where(position >= GY, from_west, 0.0),
        jnp.where(position < cell_count - GY, from_east, 0.0),
        1.0 - from_south - from_north,
        jnp.where(across_pos > 0, from_south, 0.0),
        jnp.where(across_pos < GY - 1, from_north, 0.0),
    ]
    return jnp.stack([jnp.where(inside, w, 0.0) for w in stacked])


def advance(field, weights):
    count = field.shape[0]
    here = weights[:, GY:-GY, None]
    along_x = (
        here[0] * field[GY : count - GY]
        + here[1] * field[: count - 2 * GY]
        + here[2] * field[2 * GY :]
    )
    zero_line = jnp.zeros_like(along_x[:1])
    prior_y = jnp.concatenate([zero_line, along_x[:-1]], axis=0)
    next_y = jnp.concatenate([along_x[1:], zero_line], axis=0)
    return here[3] * along_x + here[4] * prior_y + here[5] * next_y


def propagate(field, weights):
    for _ in range(STEPS):
        field = advance(field, weights)
        weights = weights[:, GY:-GY]
    return field


def shifted(block, axis, step):
    count = lax.axis_size(axis)
    return lax.ppermute(
        block, axis, [(i, i + step) for i in range(count) if 0 <= i + step < count]
    )


def body(covariance, process_noise, wind_heading, wind_speed, mixing_index):
    rows, cols = covariance.shape
    codes = (wind_heading, wind_speed, mixing_index)
    cells = wind_heading.shape[0]
    above = shifted(covariance[rows - HALO :], "row", 1)
    below = shifted(covariance[:HALO], "row", -1)
    row_weights = window_weights(
        codes, lax.axis_index("row") * rows - HALO, rows + 2 * HALO, cells
    )
    col_weights = window_weights(
        codes, lax.axis_index("col") * cols - HALO, cols + 2 * HALO, cells
    )
    inner = propagate(covariance, row_weights[:, HALO : HALO + rows])
    inner_left = shifted(inner, "col", 1)
    inner_right = shifted(inner, "col", -1)
    top = propagate(
        jnp.concatenate([above, covariance[: 2 * HALO]], axis=0), row_weights[:, : 3 * HALO]
    )
    bottom = propagate(
        jnp.concatenate([covariance[rows - 2 * HALO :], below], axis=0),
        row_weights[:, rows - HALO :],
    )
    outer = jnp.concatenate([top, bottom], axis=0)
    outer_left = shifted(outer, "col", 1)
    outer_right = shifted(outer, "col", -1)
    spread = propagate(jnp.eye(cols + 2 * HALO, dtype=jnp.float32), col_weights)

    def apply(left, own, right):
        parts = [(own, HALO, HALO + cols), (left, 0, HALO), (right, HALO + cols, cols + 2 * HALO)]
        total = 0.0
        for part, low, high in parts:
            total = total + lax.dot_general(
                part,
                spread[:, low:high],
                (((1,), (1,)), ((), ())),
                precision=lax.Precision.HIGHEST,
            )
        return total

    inner_out = apply(inner_left, inner, inner_right)
    outer_out = apply(outer_left, outer, outer_right)
    result = jnp.concatenate([outer_out[:HALO], inner_out, outer_out[HALO:]], axis=0)
    return result + process_noise


def solution(mesh):
    return jax.shard_map(
        body,
        mesh=mesh,
        in_specs=(P("row", "col"), P("row", "col"), P(), P(), P()),
        out_specs=P("row", "col"),
        check_vma=False,
    )
```

```python
import functools

import jax
import jax.numpy as jnp
from jax import lax
from jax.experimental import pallas as pl
from jax.experimental.pallas import tpu as pltpu
from jax.sharding import PartitionSpec as P

GY = 96
STEPS = 4
HALO = STEPS * GY
LANES = 128
KINDS = 6
COL = 32
PAD = 8


def find_flows(codes, flows):
    heading, speed, mixing = [code[...] for code in codes]
    tiles = heading.shape[0]
    rate = 0.1 + 0.075 * speed.astype(jnp.float32)
    diagonal = heading % 2 == 1
    length = jnp.where(diagonal, 0.5**0.5, 1.0).astype(jnp.float32)
    cosine = jnp.where((heading == 2) | (heading == 6), 0.0, length)
    cosine = jnp.where((heading > 2) & (heading < 6), -cosine, cosine)
    sine = jnp.where((heading == 0) | (heading == 4), 0.0, length)
    sine = jnp.where(heading > 4, -sine, sine)
    flows[...] = jnp.zeros_like(flows)
    inside = pl.ds(PAD, tiles)
    flows[0, inside, :] = rate * cosine
    flows[1, inside, :] = rate * sine
    flows[2, inside, :] = 0.02 + 0.02 * mixing.astype(jnp.float32)


def line(index):
    return pl.ds(pl.multiple_of(index * GY, GY), GY)


def widen(flows, first, lines, wide, at):
    zero = jnp.zeros((1, LANES), jnp.float32)

    def one(t, _):
        for tile in (3 * t, 3 * t + 1, 3 * t + 2):
            lanes = [flows[k, pl.ds(PAD + first + tile, 1), :] for k in range(3)]
            part = jnp.concatenate(lanes + [jnp.zeros((5, LANES), jnp.float32)], axis=0).T
            east, north, mixing = [jnp.broadcast_to(part[:, k : k + 1], (LANES, LANES)) for k in range(3)]
            west_part, east_part = jnp.maximum(east, 0.0) + mixing, jnp.maximum(-east, 0.0) + mixing
            south_part, north_part = jnp.maximum(north, 0.0) + mixing, jnp.maximum(-north, 0.0) + mixing
            spot = pl.ds(pl.multiple_of(tile * LANES + at, 8), LANES)
            wide[0, spot, :] = 1.0 - west_part - east_part
            wide[1, spot, :] = west_part
            wide[2, spot, :] = east_part
            wide[3, spot, :] = 1.0 - south_part - north_part
            wide[4, spot, :] = south_part
            wide[5, spot, :] = north_part
        for g in range(4):
            edge = pl.multiple_of((4 * t + g) * GY + at, 8)
            wide[4, pl.ds(edge, 1), :] = zero
            wide[5, pl.ds(edge + GY - 1, 1), :] = zero
        return 0

    lax.fori_loop(0, lines // 4, one, 0)


def line_step(lower, middle, upper, wide, at, store):
    w = [wide[kind, line(at), :] for kind in range(KINDS)]
    for tile in range(middle.shape[1] // LANES):
        lanes = slice(tile * LANES, (tile + 1) * LANES)
        along = w[0] * middle[:, lanes] + w[1] * lower[:, lanes] + w[2] * upper[:, lanes]
        store(
            lanes,
            w[3] * along + w[4] * pltpu.roll(along, 1, 0) + w[5] * pltpu.roll(along, GY - 1, 0),
        )


def step(source, shift, target, to, wide, at, count):
    def one(pair, _):
        for g in (2 * pair, 2 * pair + 1):
            rows = [source.at[line(shift + g + k), :] for k in range(3)]

            def store(lanes, value):
                target[line(to + g), lanes] = value

            line_step(*rows, wide, at + g, store)
        return 0

    lax.fori_loop(0, count // 2, one, 0)


def inner_kernel(lines, spots, _, *refs):
    codes, (field, out, flows, wide, odd, even) = refs[:3], refs[3:]
    find_flows(codes, flows)
    widen(flows, spots[0] // COL * (lines * GY // LANES), lines, wide, 0)
    step(field, 0, odd, 0, wide, 1, lines - 2)
    step(odd, 0, even, 0, wide, 2, lines - 4)
    step(even, 0, odd, 0, wide, 3, lines - 6)
    step(odd, 0, out, 0, wide, 4, lines - 8)


def outer_kernel(first, above, lines, spots, *refs):
    codes, (halo, field, out, flows, wide, odd, even) = refs[:3], refs[3:]
    find_flows(codes, flows)
    widen(flows, spots[0] // COL * (lines * GY // LANES) + first, 3 * STEPS, wide, 0)
    low = 0 if above else lines - 2 * STEPS

    def ext(index):
        if above:
            return halo.at[line(index), :] if index < STEPS else field.at[line(index - STEPS), :]
        if index < 2 * STEPS:
            return field.at[line(low + index), :]
        return halo.at[line(index - 2 * STEPS), :]

    seam = STEPS if above else 2 * STEPS
    for g in (seam - 2, seam - 1):

        def store(lanes, value):
            odd[line(g), lanes] = value

        line_step(ext(g), ext(g + 1), ext(g + 2), wide, g + 1, store)
    if above:
        step(halo, 0, odd, 0, wide, 1, 2)
        step(field, 0, odd, 4, wide, 5, 6)
    else:
        step(field, low, odd, 0, wide, 1, 6)
        step(halo, 0, odd, 8, wide, 9, 2)
    step(odd, 0, even, 0, wide, 2, 8)
    step(even, 0, odd, 0, wide, 3, 6)
    step(odd, 0, out, 0, wide, 4, 4)


def adjoint_kernel(spots, *refs):
    codes, (out_high, out_low, flows, wide, held, field) = refs[:3], refs[3:]
    cols = field.shape[1]
    tiles = [slice(tile * LANES, (tile + 1) * LANES) for tile in range(cols // LANES)]
    lines = 3 * STEPS
    find_flows(codes, flows)
    widen(flows, (spots[0] % COL - 1) * (HALO // LANES), lines, wide, GY)
    zero = jnp.zeros((GY, LANES), jnp.float32)
    for kind in range(KINDS):
        wide[kind, :GY, :] = zero
        wide[kind, GY + lines * GY :, :] = zero
    held[...] = jnp.zeros_like(held)
    place = lax.broadcasted_iota(jnp.int32, (HALO, cols), 0)
    lane = lax.broadcasted_iota(jnp.int32, (HALO, cols), 1)
    field[HALO : 2 * HALO, :] = jnp.where(place == lane, 1.0, 0.0).astype(jnp.float32)
    for number in range(STEPS):
        low, high = STEPS - number, 2 * STEPS + number

        def across(pair, _):
            for g in (2 * pair, 2 * pair + 1):
                w = [wide[kind, line(low + g + 1), :] for kind in (3, 4, 5)]
                for lanes in tiles:
                    here = field[line(low + g), lanes]
                    held[line(low + g + 1), lanes] = (
                        w[0] * here + pltpu.roll(w[1] * here, GY - 1, 0) + pltpu.roll(w[2] * here, 1, 0)
                    )
            return 0

        def along(pair, _):
            for g in (2 * pair, 2 * pair + 1):
                w = [wide[kind, line(low + g + at), :] for kind, at in ((0, 0), (1, 1), (2, -1))]
                for lanes in tiles:
                    new = (
                        w[0] * held[line(low + g), lanes]
                        + w[1] * held[line(low + g + 1), lanes]
                        + w[2] * held[line(low + g - 1), lanes]
                    )
                    if number == STEPS - 1:
                        high_part = new.astype(jnp.bfloat16)
                        out_high[line(low + g - 1), lanes] = high_part
                        out_low[line(low + g - 1), lanes] = (new - high_part.astype(jnp.float32)).astype(
                            jnp.bfloat16
                        )
                    else:
                        field[line(low + g - 1), lanes] = new
            return 0

        lax.fori_loop(0, (high - low) // 2, across, 0)
        lax.fori_loop(0, (high - low + 2) // 2, along, 0)


def dot(field, spread_high, spread_low, index):
    part = pl.ds(pl.multiple_of(index * HALO, HALO), HALO)
    high = field.astype(jnp.bfloat16)
    low = (field - high.astype(jnp.float32)).astype(jnp.bfloat16)
    product = functools.partial(jnp.dot, preferred_element_type=jnp.float32)
    return product(high, spread_high[part, :]) + (
        product(low, spread_high[part, :]) + product(high, spread_low[part, :])
    )


def own_kernel(spots, field, field_on, spread_high, spread_low, noise, out):
    out[...] = (
        noise[...]
        + dot(field[...], spread_high, spread_low, 1)
        + dot(field_on[...], spread_high, spread_low, 2 - 2 * (spots[0] % 2))
    )


def inner_last_kernel(spots, field, field_on, field_off, spread_high, spread_low, noise, out):
    out[...] = (
        noise[...]
        + dot(field[...], spread_high, spread_low, 1)
        + dot(field_on[...], spread_high, spread_low, 2 - 2 * (spots[0] % 2))
        + dot(field_off[...], spread_high, spread_low, 2 * (spots[0] % 2))
    )


def last_kernel(spots, field_off, spread_high, spread_low, base, _, out):
    out[...] = base[...] + dot(field_off[...], spread_high, spread_low, 2 * (spots[0] % 2))


def cost(flops, moved):
    return pl.CostEstimate(flops=flops, bytes_accessed=moved, transcendentals=0)


def shape(*dims):
    return jax.ShapeDtypeStruct(dims, jnp.float32)


def scratch(*dims):
    return pltpu.VMEM(dims, jnp.float32)


def shifted(block, axis, pairs):
    count = lax.axis_size(axis)
    return lax.ppermute(block, axis, [(i, j) for i, j in map(pairs, range(count)) if 0 <= j < count])


HERE = pl.BlockSpec(memory_space=pltpu.VMEM)
SCALARS = pl.BlockSpec(memory_space=pltpu.SMEM)
SUB = 192
ROOM = pltpu.CompilerParams(vmem_limit_bytes=20 << 20)


def near(array):
    return pltpu.with_memory_space_constraint(array, pltpu.VMEM)


def body(covariance, process_noise, wind_heading, wind_speed, mixing_index):
    rows, cols = covariance.shape
    lines = rows // GY
    codes = [code.reshape(-1, LANES) for code in (wind_heading, wind_speed, mixing_index)]
    place = lax.axis_index("row") * lax.axis_size("col") + lax.axis_index("col")
    spots = place.astype(jnp.int32).reshape(1)
    flow_room = scratch(3, 2 * PAD + codes[0].shape[0], LANES)
    on_pairs = lambda i: (i, i ^ 1)
    off_pairs = lambda i: (i, i + 1 if i % 2 else i - 1)

    above = shifted(covariance[rows - HALO :], "row", lambda i: (i, i + 1))
    below = shifted(covariance[:HALO], "row", lambda i: (i, i - 1))
    near_field = near(covariance)
    spread = pl.pallas_call(
        adjoint_kernel,
        in_specs=[SCALARS, HERE, HERE, HERE],
        out_specs=[HERE, HERE],
        out_shape=[jax.ShapeDtypeStruct((3 * HALO, cols), jnp.bfloat16)] * 2,
        scratch_shapes=[
            flow_room,
            scratch(KINDS, 3 * HALO + 2 * GY, LANES),
            scratch(3 * HALO + 2 * GY, cols),
            scratch(3 * HALO, cols),
        ],
        cost_estimate=cost(2 * 6 * 4 * 3 * HALO * cols, 4 * 3 * HALO * cols),
        compiler_params=ROOM,
        name="spread",
    )(spots, *codes)
    spread = [near(part) for part in spread]
    inner = pl.pallas_call(
        functools.partial(inner_kernel, lines),
        in_specs=[SCALARS, pl.BlockSpec(memory_space=pl.ANY), HERE, HERE, HERE, HERE],
        out_specs=HERE,
        out_shape=shape(2 * HALO, cols),
        scratch_shapes=[flow_room, scratch(KINDS, rows, LANES), scratch(rows, cols), scratch(rows, cols)],
        cost_estimate=cost(2 * 6 * 4 * rows * cols, 4 * 2 * rows * cols),
        compiler_params=ROOM,
        name="inner",
    )(spots, spread[1], *codes, near_field)
    inner_off = shifted(inner, "col", off_pairs)
    inner_on = shifted(inner, "col", on_pairs)

    def outer_part(halo, first, is_above):
        return pl.pallas_call(
            functools.partial(outer_kernel, first, is_above, lines),
            in_specs=[SCALARS] + [HERE] * 5,
            out_specs=HERE,
            out_shape=shape(HALO, cols),
            scratch_shapes=[
                flow_room,
                scratch(KINDS, 3 * HALO, LANES),
                scratch(3 * HALO, cols),
                scratch(3 * HALO, cols),
            ],
            cost_estimate=cost(6 * 4 * rows * cols, 4 * rows * cols),
            compiler_params=ROOM,
        )(spots, *codes, near(halo), near_field)

    def call(kernel, fields, base, base_at, out_rows, out_at, count, onto=None):
        part = lambda at: pl.BlockSpec((SUB, cols), lambda i, spots: (i + at, 0))
        onto = () if onto is None else (onto,)
        moved = 4 * count * SUB * cols * (len(fields) + 2)
        return pl.pallas_call(
            kernel,
            grid_spec=pltpu.PrefetchScalarGridSpec(
                num_scalar_prefetch=1,
                grid=(count,),
                in_specs=[part(0)] * len(fields)
                + [HERE, HERE, part(base_at)]
                + [pl.BlockSpec(memory_space=pl.ANY)] * len(onto),
                out_specs=part(out_at),
            ),
            out_shape=shape(out_rows, cols),
            input_output_aliases={len(fields) + 4: 0} if onto else {},
            cost_estimate=cost(6 * count * SUB * cols * HALO * len(fields), moved),
            compiler_params=ROOM,
        )(spots, *fields, *spread, base, *onto)

    top = outer_part(above, -HALO // LANES, True)
    top_off = shifted(top, "col", off_pairs)
    top_on = shifted(top, "col", on_pairs)
    bottom = outer_part(below, (rows - 2 * HALO) // LANES, False)
    bottom_off = shifted(bottom, "col", off_pairs)
    bottom_on = shifted(bottom, "col", on_pairs)
    low, high = HALO // SUB, (rows - HALO) // SUB
    result = call(inner_last_kernel, [inner, inner_on, inner_off], process_noise, low, rows, low, high - low)
    top_base = call(own_kernel, [top, top_on], process_noise, 0, HALO, 0, low)
    bottom_base = call(own_kernel, [bottom, bottom_on], process_noise, high, HALO, 0, low)
    result = call(last_kernel, [top_off], top_base, 0, rows, 0, low, result)
    return call(last_kernel, [bottom_off], bottom_base, 0, rows, high, low, result)


def solution(mesh):
    return jax.shard_map(
        body,
        mesh=mesh,
        in_specs=(P("row", "col"), P("row", "col"), P(), P(), P()),
        out_specs=P("row", "col"),
        check_vma=False,
    )
```

```python
import functools

import jax
import jax.numpy as jnp
from jax import lax
from jax.experimental import pallas as pl
from jax.experimental.pallas import tpu as pltpu
from jax.sharding import PartitionSpec as P

GY = 96
STEPS = 4
HALO = STEPS * GY
LANES = 128
KINDS = 6
COL = 32
PAD = 8


def find_flows(codes, flows):
    heading, speed, mixing = [code[...] for code in codes]
    tiles = heading.shape[0]
    rate = 0.1 + 0.075 * speed.astype(jnp.float32)
    diagonal = heading % 2 == 1
    length = jnp.where(diagonal, 0.5**0.5, 1.0).astype(jnp.float32)
    cosine = jnp.where((heading == 2) | (heading == 6), 0.0, length)
    cosine = jnp.where((heading > 2) & (heading < 6), -cosine, cosine)
    sine = jnp.where((heading == 0) | (heading == 4), 0.0, length)
    sine = jnp.where(heading > 4, -sine, sine)
    flows[...] = jnp.zeros_like(flows)
    inside = pl.ds(PAD, tiles)
    flows[0, inside, :] = rate * cosine
    flows[1, inside, :] = rate * sine
    flows[2, inside, :] = 0.02 + 0.02 * mixing.astype(jnp.float32)


def line(index):
    return pl.ds(pl.multiple_of(index * GY, GY), GY)


def widen(flows, first, lines, wide, at):
    zero = jnp.zeros((1, LANES), jnp.float32)

    def one(t, _):
        for tile in (3 * t, 3 * t + 1, 3 * t + 2):
            lanes = [flows[k, pl.ds(PAD + first + tile, 1), :] for k in range(3)]
            part = jnp.concatenate(lanes + [jnp.zeros((5, LANES), jnp.float32)], axis=0).T
            east, north, mixing = [jnp.broadcast_to(part[:, k : k + 1], (LANES, LANES)) for k in range(3)]
            west_part, east_part = jnp.maximum(east, 0.0) + mixing, jnp.maximum(-east, 0.0) + mixing
            south_part, north_part = jnp.maximum(north, 0.0) + mixing, jnp.maximum(-north, 0.0) + mixing
            spot = pl.ds(pl.multiple_of(tile * LANES + at, 8), LANES)
            wide[0, spot, :] = 1.0 - west_part - east_part
            wide[1, spot, :] = west_part
            wide[2, spot, :] = east_part
            wide[3, spot, :] = 1.0 - south_part - north_part
            wide[4, spot, :] = south_part
            wide[5, spot, :] = north_part
        for g in range(4):
            edge = pl.multiple_of((4 * t + g) * GY + at, 8)
            wide[4, pl.ds(edge, 1), :] = zero
            wide[5, pl.ds(edge + GY - 1, 1), :] = zero
        return 0

    lax.fori_loop(0, lines // 4, one, 0)


def line_step(rows, wide, at, store, tiles):
    w = [wide[kind, line(at), :] for kind in range(KINDS)]
    for tile in range(tiles):
        lower, middle, upper = [
            ref[line(number), pl.ds(skip + tile * LANES, LANES)] for ref, number, skip in rows
        ]
        along = w[0] * middle + w[1] * lower + w[2] * upper
        store(
            slice(tile * LANES, (tile + 1) * LANES),
            w[3] * along + w[4] * pltpu.roll(along, 1, 0) + w[5] * pltpu.roll(along, GY - 1, 0),
        )


def step(source, shift, target, to, wide, at, count, skip=0):
    def one(pair, _):
        for g in (2 * pair, 2 * pair + 1):

            def store(lanes, value):
                target[line(to + g), lanes] = value

            line_step(
                [(source, shift + g + k, skip) for k in range(3)], wide, at + g, store, target.shape[1] // LANES
            )
        return 0

    lax.fori_loop(0, count // 2, one, 0)


def cut_kernel(pieces, spots, field, *refs):
    outs, sems = refs[: len(pieces)], refs[len(pieces)]
    odd = spots[0] // COL % 2
    for number, (row, lane) in enumerate(pieces):
        out = outs[number]
        rows, lanes = out.shape

        def copy(start):
            part = field.at[pl.ds(start, rows), pl.ds(lane, lanes)]
            return pltpu.make_async_copy(part, out, sems.at[number])

        if row in ("outer", "inner"):
            side = odd if row == "outer" else 1 - odd
            copy(pl.multiple_of(side * (field.shape[0] - rows), 8)).start()
        else:
            copy(row).start()
    for number, (row, lane) in enumerate(pieces):
        out = outs[number]
        part = field.at[pl.ds(0, out.shape[0]), pl.ds(lane, out.shape[1])]
        pltpu.make_async_copy(part, out, sems.at[number]).wait()


def weights_kernel(lines, spots, *refs):
    codes, (wide, flows) = refs[:3], refs[3:]
    find_flows(codes, flows)
    pair = spots[0] // COL // 2
    widen(flows, pair * (2 * lines * GY // LANES) - HALO // LANES, 2 * lines + 2 * STEPS, wide, 0)


def block_kernel(mode, lane, spots, wide, far, field, other, out, *refs):
    full, odd, even = refs[-3:]
    rows = field.shape[0]
    lines = rows // GY
    lanes = slice(lane, lane + LANES)
    index = spots[0] // COL
    upper, lower, every = slice(0, HALO), slice(rows - HALO, rows), slice(0, LANES)
    full[HALO : HALO + rows, :] = other[...] if mode == "passed" else field[:, lanes]
    if mode == "own":
        full[:HALO, :] = far[...]
        full[HALO + rows :, :] = other[...]
    else:
        block = index + 1 if mode == "passed" else index
        next_ref, next_lanes = (field, lanes) if mode == "passed" else (other, every)
        far_lanes = lanes if mode == "passed" else every

        @pl.when(block % 2 == 0)
        def _():
            full[:HALO, :] = far[:, far_lanes]
            full[HALO + rows :, :] = next_ref[upper, next_lanes]
            if mode == "passed":
                refs[0][...] = other[upper, :]

        @pl.when(block % 2 == 1)
        def _():
            full[:HALO, :] = next_ref[lower, next_lanes]
            full[HALO + rows :, :] = far[:, far_lanes]
            if mode == "passed":
                refs[0][...] = other[lower, :]

    at = ((index + 1 if mode == "passed" else index) % 2) * lines
    step(full, 0, odd, 0, wide, at + 1, lines + 6)
    step(odd, 0, even, 0, wide, at + 2, lines + 4)
    step(even, 0, odd, 0, wide, at + 3, lines + 2)
    step(odd, 0, out, 0, wide, at + 4, lines)


def adjoint_kernel(spots, *refs):
    codes, (out_high, out_low, flows, wide, held, field) = refs[:3], refs[3:]
    cols = field.shape[1]
    tiles = [slice(tile * LANES, (tile + 1) * LANES) for tile in range(cols // LANES)]
    lines = 3 * STEPS
    find_flows(codes, flows)
    widen(flows, (spots[0] % COL - 1) * (HALO // LANES), lines, wide, GY)
    zero = jnp.zeros((GY, LANES), jnp.float32)
    for kind in range(KINDS):
        wide[kind, :GY, :] = zero
        wide[kind, GY + lines * GY :, :] = zero
    held[...] = jnp.zeros_like(held)
    place = lax.broadcasted_iota(jnp.int32, (HALO, cols), 0)
    lane = lax.broadcasted_iota(jnp.int32, (HALO, cols), 1)
    field[HALO : 2 * HALO, :] = jnp.where(place == lane, 1.0, 0.0).astype(jnp.float32)
    for number in range(STEPS):
        low, high = STEPS - number, 2 * STEPS + number

        def across(pair, _):
            for g in (2 * pair, 2 * pair + 1):
                w = [wide[kind, line(low + g + 1), :] for kind in (3, 4, 5)]
                for lanes in tiles:
                    here = field[line(low + g), lanes]
                    held[line(low + g + 1), lanes] = (
                        w[0] * here + pltpu.roll(w[1] * here, GY - 1, 0) + pltpu.roll(w[2] * here, 1, 0)
                    )
            return 0

        def along(pair, _):
            for g in (2 * pair, 2 * pair + 1):
                w = [wide[kind, line(low + g + at), :] for kind, at in ((0, 0), (1, 1), (2, -1))]
                for lanes in tiles:
                    new = (
                        w[0] * held[line(low + g), lanes]
                        + w[1] * held[line(low + g + 1), lanes]
                        + w[2] * held[line(low + g - 1), lanes]
                    )
                    if number == STEPS - 1:
                        high_part = new.astype(jnp.bfloat16)
                        out_high[line(low + g - 1), lanes] = high_part
                        out_low[line(low + g - 1), lanes] = (new - high_part.astype(jnp.float32)).astype(
                            jnp.bfloat16
                        )
                    else:
                        field[line(low + g - 1), lanes] = new
            return 0

        lax.fori_loop(0, (high - low) // 2, across, 0)
        lax.fori_loop(0, (high - low + 2) // 2, along, 0)


def product_kernel(terms, spots, *refs):
    count = len(terms)
    fields, (spread_high, spread_low, base) = refs[:count], refs[count : count + 3]
    out, held = refs[-2:]

    @pl.when(pl.program_id(0) == 0)
    def _():
        off = 2 * (spots[0] % 2)
        for number, (kind, lane) in enumerate(terms):
            index = {"own": 1, "on": 2 - off, "off": off}[kind]
            part = pl.ds(pl.multiple_of(index * HALO + lane, LANES), LANES)
            for at, spread in enumerate((spread_high, spread_high, spread_low)):
                first = (at * count + number) * LANES
                held[first : first + LANES, :] = spread[part, :]

    rows = pl.ds(pl.multiple_of(pl.program_id(0) * SUB, SUB), SUB)
    values = [field[rows, :] for field in fields]
    high = [value.astype(jnp.bfloat16) for value in values]
    low = [(value - part.astype(jnp.float32)).astype(jnp.bfloat16) for value, part in zip(values, high)]
    into = rows if out.shape[0] > SUB else slice(None)
    out[into, :] = base[rows, :] + jnp.dot(
        jnp.concatenate(high + low + high, axis=1), held[...], preferred_element_type=jnp.float32
    )


def cost(flops, moved):
    return pl.CostEstimate(flops=flops, bytes_accessed=moved, transcendentals=0)


def shape(*dims):
    return jax.ShapeDtypeStruct(dims, jnp.float32)


def scratch(*dims):
    return pltpu.VMEM(dims, jnp.float32)


def shifted(block, axis, pairs):
    count = lax.axis_size(axis)
    return lax.ppermute(block, axis, [(i, j) for i, j in map(pairs, range(count)) if 0 <= j < count])


HERE = pl.BlockSpec(memory_space=pltpu.VMEM)
SCALARS = pl.BlockSpec(memory_space=pltpu.SMEM)
SUB = 384
ROOM = pltpu.CompilerParams(vmem_limit_bytes=14 << 20)


WIDE_ROOM = pltpu.CompilerParams(vmem_limit_bytes=18 << 20)


def near(array):
    return pltpu.with_memory_space_constraint(array, pltpu.VMEM)


def body(covariance, process_noise, wind_heading, wind_speed, mixing_index):
    rows, cols = covariance.shape
    lines = rows // GY
    codes = [code.reshape(-1, LANES) for code in (wind_heading, wind_speed, mixing_index)]
    place = lax.axis_index("row") * lax.axis_size("col") + lax.axis_index("col")
    spots = place.astype(jnp.int32).reshape(1)
    flow_room = scratch(3, 2 * PAD + codes[0].shape[0], LANES)
    on_pairs = lambda i: (i, i ^ 1)
    off_pairs = lambda i: (i, i + 1 if i % 2 else i - 1)

    def relay_off_pairs():
        count = lax.axis_size("col")
        pairs = [off_pairs(i) for i in range(count)]
        return [
            (r * count + i, (r ^ 1) * count + j)
            for r in range(lax.axis_size("row"))
            for i, j in pairs
            if 0 <= j < count
        ]

    def cut(source, pieces, shapes, space):
        return pl.pallas_call(
            functools.partial(cut_kernel, pieces),
            in_specs=[SCALARS, pl.BlockSpec(memory_space=space)],
            out_specs=[HERE] * len(pieces),
            out_shape=[shape(*dims) for dims in shapes],
            scratch_shapes=[pltpu.SemaphoreType.DMA((len(pieces),))],
            cost_estimate=cost(0, 1 << 22),
            compiler_params=ROOM,
        )(spots, source)

    chunks = range(0, cols, LANES)
    late = chunks[-1]
    hbm = pltpu.HBM
    raw_0, raw_late, edge = cut(
        covariance, [(0, 0), (0, late), ("outer", 0)], [(rows, LANES), (rows, LANES), (HALO, late)], hbm
    )
    swap = lambda piece: shifted(piece, "row", lambda i: (i, i ^ 1))
    x_out = lambda i: (i, i + 2 if i % 2 else i - 2)
    x_in = lambda i: (i, i - 2 if i % 2 else i + 2)
    swapped = [swap(raw_0)]
    crossed = lax.ppermute(raw_late, ("row", "col"), relay_off_pairs())
    far_other = shifted(edge, "row", x_out)
    raw_1, above, below = cut(
        covariance, [(0, LANES), (rows - HALO, late), (0, late)], [(rows, LANES), (HALO, LANES), (HALO, LANES)], hbm
    )
    swapped.append(swap(raw_1))
    above = shifted(above, "row", lambda i: (i, i + 1))
    below = shifted(below, "row", lambda i: (i, i - 1))
    near_field = near(covariance)
    spread = pl.pallas_call(
        adjoint_kernel,
        in_specs=[SCALARS, HERE, HERE, HERE],
        out_specs=[HERE, HERE],
        out_shape=[jax.ShapeDtypeStruct((3 * HALO, cols), jnp.bfloat16)] * 2,
        scratch_shapes=[
            flow_room,
            scratch(KINDS, 3 * HALO + 2 * GY, LANES),
            scratch(3 * HALO + 2 * GY, cols),
            scratch(3 * HALO, cols),
        ],
        cost_estimate=cost(2 * 6 * 4 * 3 * HALO * cols, 4 * 3 * HALO * cols),
        compiler_params=ROOM,
        name="spread",
    )(spots, *codes)
    spread = [near(part) for part in spread]
    long = rows + 2 * HALO
    wide = pl.pallas_call(
        functools.partial(weights_kernel, lines),
        in_specs=[SCALARS] + [HERE] * 3,
        out_specs=HERE,
        out_shape=shape(KINDS, rows + long, LANES),
        scratch_shapes=[flow_room],
        cost_estimate=cost(0, 1 << 24),
        compiler_params=WIDE_ROOM,
        name="weights",
    )(spots, *codes)

    def block_part(mode, lane, far, field, other):
        outs = [shape(rows, LANES)] + ([shape(HALO, LANES)] if mode == "passed" else [])
        return pl.pallas_call(
            functools.partial(block_kernel, mode, lane),
            in_specs=[SCALARS] + [HERE] * 4,
            out_specs=[HERE] * len(outs),
            out_shape=outs,
            scratch_shapes=[scratch(long, LANES)] * 3,
            cost_estimate=cost(6 * 4 * rows * cols, 4 * rows * cols),
            compiler_params=ROOM,
        )(spots, near(wide), near(far), near(field), near(other))

    def call(terms, base, final=False):
        width = LANES * len(terms)
        moved = 4 * rows * (width + 2 * cols)
        return pl.pallas_call(
            functools.partial(product_kernel, [(kind, lane) for _, kind, lane in terms]),
            grid=(rows // SUB,),
            in_specs=[SCALARS] + [HERE] * (len(terms) + 3),
            out_specs=pl.BlockSpec((SUB, cols), lambda i: (i, 0)) if final else HERE,
            out_shape=shape(rows, cols),
            scratch_shapes=[pltpu.VMEM((3 * width, cols), jnp.bfloat16)],
            cost_estimate=cost(6 * rows * cols * width, moved),
            compiler_params=ROOM,
        )(spots, *[near(field) for field, _, _ in terms], *spread, near(base))

    kept, kept_on, relayed = [], [], []
    for number, other in enumerate(swapped):
        lane = chunks[number]
        passed, back = block_part("passed", lane, far_other, near_field, other)
        relayed.append(lax.ppermute(passed, ("row", "col"), relay_off_pairs()))
        far_mine = shifted(back, "row", x_in)
        kept += block_part("kept", lane, far_mine, near_field, other)
        kept_on.append(shifted(kept[-1], "col", on_pairs))
    turned = swap(crossed)
    (crossed_edge,) = cut(crossed, [("inner", 0)], [(HALO, LANES)], pl.ANY)
    far_off = shifted(crossed_edge, "row", x_in)
    kept += block_part("own", late, above, near_field, below)
    kept_on.append(shifted(kept[-1], "col", on_pairs))
    relayed += block_part("off", 0, far_off, turned, crossed)

    def near_terms(number):
        lane = chunks[number]
        return [(kept[number], "own", lane), (kept_on[number], "on", lane)]

    def far_terms(number):
        return [(relayed[number], "off", chunks[number])]

    result = call(near_terms(0), process_noise)
    result = call(near_terms(1) + far_terms(0), result)
    return call(near_terms(2) + far_terms(1) + far_terms(2), result, True)


def solution(mesh):
    return jax.shard_map(
        body,
        mesh=mesh,
        in_specs=(P("row", "col"), P("row", "col"), P(), P(), P()),
        out_specs=P("row", "col"),
        check_vma=False,
    )
```

```python
import functools

import jax
import jax.numpy as jnp
from jax import lax
from jax.experimental import pallas as pl
from jax.experimental.pallas import tpu as pltpu
from jax.sharding import PartitionSpec as P

GY = 96
STEPS = 4
HALO = STEPS * GY
LANES = 128
KINDS = 6
COL = 32
PAD = 8


def find_flows(codes, flows):
    heading, speed, mixing = [code[...] for code in codes]
    tiles = heading.shape[0]
    rate = 0.1 + 0.075 * speed.astype(jnp.float32)
    diagonal = heading % 2 == 1
    length = jnp.where(diagonal, 0.5**0.5, 1.0).astype(jnp.float32)
    cosine = jnp.where((heading == 2) | (heading == 6), 0.0, length)
    cosine = jnp.where((heading > 2) & (heading < 6), -cosine, cosine)
    sine = jnp.where((heading == 0) | (heading == 4), 0.0, length)
    sine = jnp.where(heading > 4, -sine, sine)
    flows[...] = jnp.zeros_like(flows)
    inside = pl.ds(PAD, tiles)
    flows[0, inside, :] = rate * cosine
    flows[1, inside, :] = rate * sine
    flows[2, inside, :] = 0.02 + 0.02 * mixing.astype(jnp.float32)


def line(index):
    return pl.ds(pl.multiple_of(index * GY, GY), GY)


def widen(flows, first, lines, wide, at):
    zero = jnp.zeros((1, LANES), jnp.float32)

    def one(t, _):
        for tile in (3 * t, 3 * t + 1, 3 * t + 2):
            lanes = [flows[k, pl.ds(PAD + first + tile, 1), :] for k in range(3)]
            part = jnp.concatenate(lanes + [jnp.zeros((5, LANES), jnp.float32)], axis=0).T
            east, north, mixing = [jnp.broadcast_to(part[:, k : k + 1], (LANES, LANES)) for k in range(3)]
            west_part, east_part = jnp.maximum(east, 0.0) + mixing, jnp.maximum(-east, 0.0) + mixing
            south_part, north_part = jnp.maximum(north, 0.0) + mixing, jnp.maximum(-north, 0.0) + mixing
            spot = pl.ds(pl.multiple_of(tile * LANES + at, 8), LANES)
            wide[0, spot, :] = 1.0 - west_part - east_part
            wide[1, spot, :] = west_part
            wide[2, spot, :] = east_part
            wide[3, spot, :] = 1.0 - south_part - north_part
            wide[4, spot, :] = south_part
            wide[5, spot, :] = north_part
        for g in range(4):
            edge = pl.multiple_of((4 * t + g) * GY + at, 8)
            wide[4, pl.ds(edge, 1), :] = zero
            wide[5, pl.ds(edge + GY - 1, 1), :] = zero
        return 0

    lax.fori_loop(0, lines // 4, one, 0)


def line_step(rows, wide, at, store, tiles):
    w = [wide[kind, line(at), :] for kind in range(KINDS)]
    for tile in range(tiles):
        lower, middle, upper = [
            ref[line(number), pl.ds(skip + tile * LANES, LANES)] for ref, number, skip in rows
        ]
        along = w[0] * middle + w[1] * lower + w[2] * upper
        store(
            slice(tile * LANES, (tile + 1) * LANES),
            w[3] * along + w[4] * pltpu.roll(along, 1, 0) + w[5] * pltpu.roll(along, GY - 1, 0),
        )


def step(source, shift, target, to, wide, at, count, skip=0):
    def one(pair, _):
        for g in (2 * pair, 2 * pair + 1):

            def store(lanes, value):
                target[line(to + g), lanes] = value

            line_step(
                [(source, shift + g + k, skip) for k in range(3)], wide, at + g, store, target.shape[1] // LANES
            )
        return 0

    lax.fori_loop(0, count // 2, one, 0)


def cut_kernel(pieces, spots, field, *refs):
    outs, sems = refs[: len(pieces)], refs[len(pieces)]
    odd = spots[0] // COL % 2
    for number, (row, lane) in enumerate(pieces):
        out = outs[number]
        rows, lanes = out.shape

        def copy(start):
            part = field.at[pl.ds(start, rows), pl.ds(lane, lanes)]
            return pltpu.make_async_copy(part, out, sems.at[number])

        if row in ("outer", "inner"):
            side = odd if row == "outer" else 1 - odd
            copy(pl.multiple_of(side * (field.shape[0] - rows), 8)).start()
        else:
            copy(row).start()
    for number, (row, lane) in enumerate(pieces):
        out = outs[number]
        part = field.at[pl.ds(0, out.shape[0]), pl.ds(lane, out.shape[1])]
        pltpu.make_async_copy(part, out, sems.at[number]).wait()


def weights_kernel(lines, spots, *refs):
    codes, (wide, flows) = refs[:3], refs[3:]
    find_flows(codes, flows)
    pair = spots[0] // COL // 2
    widen(flows, pair * (2 * lines * GY // LANES) - HALO // LANES, 2 * lines + 2 * STEPS, wide, 0)


def block_kernel(mode, lane, spots, wide, far, field, other, out, *refs):
    full, odd, even = refs[-3:]
    rows = field.shape[0]
    lines = rows // GY
    lanes = slice(lane, lane + LANES)
    index = spots[0] // COL
    upper, lower, every = slice(0, HALO), slice(rows - HALO, rows), slice(0, LANES)
    full[HALO : HALO + rows, :] = other[...] if mode == "passed" else field[:, lanes]
    if mode == "own":
        full[:HALO, :] = far[...]
        full[HALO + rows :, :] = other[...]
    else:
        block = index + 1 if mode == "passed" else index
        next_ref, next_lanes = (field, lanes) if mode == "passed" else (other, every)
        far_lanes = lanes if mode == "passed" else every

        @pl.when(block % 2 == 0)
        def _():
            full[:HALO, :] = far[:, far_lanes]
            full[HALO + rows :, :] = next_ref[upper, next_lanes]
            if mode == "passed":
                refs[0][...] = other[upper, :]

        @pl.when(block % 2 == 1)
        def _():
            full[:HALO, :] = next_ref[lower, next_lanes]
            full[HALO + rows :, :] = far[:, far_lanes]
            if mode == "passed":
                refs[0][...] = other[lower, :]

    at = ((index + 1 if mode == "passed" else index) % 2) * lines
    step(full, 0, odd, 0, wide, at + 1, lines + 6)
    step(odd, 0, even, 0, wide, at + 2, lines + 4)
    step(even, 0, odd, 0, wide, at + 3, lines + 2)
    step(odd, 0, out, 0, wide, at + 4, lines)


def adjoint_kernel(spots, *refs):
    codes, (out_high, out_low, flows, wide, held, field) = refs[:3], refs[3:]
    cols = field.shape[1]
    tiles = [slice(tile * LANES, (tile + 1) * LANES) for tile in range(cols // LANES)]
    lines = 3 * STEPS
    find_flows(codes, flows)
    widen(flows, (spots[0] % COL - 1) * (HALO // LANES), lines, wide, GY)
    zero = jnp.zeros((GY, LANES), jnp.float32)
    for kind in range(KINDS):
        wide[kind, :GY, :] = zero
        wide[kind, GY + lines * GY :, :] = zero
    held[...] = jnp.zeros_like(held)
    place = lax.broadcasted_iota(jnp.int32, (HALO, cols), 0)
    lane = lax.broadcasted_iota(jnp.int32, (HALO, cols), 1)
    field[HALO : 2 * HALO, :] = jnp.where(place == lane, 1.0, 0.0).astype(jnp.float32)
    for number in range(STEPS):
        low, high = STEPS - number, 2 * STEPS + number

        def across(pair, _):
            for g in (2 * pair, 2 * pair + 1):
                w = [wide[kind, line(low + g + 1), :] for kind in (3, 4, 5)]
                for lanes in tiles:
                    here = field[line(low + g), lanes]
                    held[line(low + g + 1), lanes] = (
                        w[0] * here + pltpu.roll(w[1] * here, GY - 1, 0) + pltpu.roll(w[2] * here, 1, 0)
                    )
            return 0

        def along(pair, _):
            for g in (2 * pair, 2 * pair + 1):
                w = [wide[kind, line(low + g + at), :] for kind, at in ((0, 0), (1, 1), (2, -1))]
                for lanes in tiles:
                    new = (
                        w[0] * held[line(low + g), lanes]
                        + w[1] * held[line(low + g + 1), lanes]
                        + w[2] * held[line(low + g - 1), lanes]
                    )
                    if number == STEPS - 1:
                        high_part = new.astype(jnp.bfloat16)
                        out_high[line(low + g - 1), lanes] = high_part
                        out_low[line(low + g - 1), lanes] = (new - high_part.astype(jnp.float32)).astype(
                            jnp.bfloat16
                        )
                    else:
                        field[line(low + g - 1), lanes] = new
            return 0

        lax.fori_loop(0, (high - low) // 2, across, 0)
        lax.fori_loop(0, (high - low + 2) // 2, along, 0)


def product_kernel(terms, spots, *refs):
    count = len(terms)
    fields, (spread_high, spread_low, base) = refs[:count], refs[count : count + 3]
    out, held = refs[-2:]

    @pl.when(pl.program_id(0) == 0)
    def _():
        off = 2 * (spots[0] % 2)
        for number, (kind, lane) in enumerate(terms):
            index = {"own": 1, "on": 2 - off, "off": off}[kind]
            part = pl.ds(pl.multiple_of(index * HALO + lane, LANES), LANES)
            for at, spread in enumerate((spread_high, spread_high, spread_low)):
                first = (at * count + number) * LANES
                held[first : first + LANES, :] = spread[part, :]

    rows = pl.ds(pl.multiple_of(pl.program_id(0) * SUB, SUB), SUB)
    values = [field[rows, :] for field in fields]
    high = [value.astype(jnp.bfloat16) for value in values]
    low = [(value - part.astype(jnp.float32)).astype(jnp.bfloat16) for value, part in zip(values, high)]
    into = rows if out.shape[0] > SUB else slice(None)
    out[into, :] = base[rows, :] + jnp.dot(
        jnp.concatenate(high + low + high, axis=1), held[...], preferred_element_type=jnp.float32
    )


def cost(flops, moved):
    return pl.CostEstimate(flops=flops, bytes_accessed=moved, transcendentals=0)


def shape(*dims):
    return jax.ShapeDtypeStruct(dims, jnp.float32)


def scratch(*dims):
    return pltpu.VMEM(dims, jnp.float32)


def shifted(block, axis, pairs):
    count = lax.axis_size(axis)
    return lax.ppermute(block, axis, [(i, j) for i, j in map(pairs, range(count)) if 0 <= j < count])


HERE = pl.BlockSpec(memory_space=pltpu.VMEM)
SCALARS = pl.BlockSpec(memory_space=pltpu.SMEM)
SUB = 384
ROOM = pltpu.CompilerParams(vmem_limit_bytes=14 << 20)


WIDE_ROOM = pltpu.CompilerParams(vmem_limit_bytes=18 << 20)


def near(array):
    return pltpu.with_memory_space_constraint(array, pltpu.VMEM)


def body(covariance, process_noise, wind_heading, wind_speed, mixing_index):
    rows, cols = covariance.shape
    lines = rows // GY
    codes = [code.reshape(-1, LANES) for code in (wind_heading, wind_speed, mixing_index)]
    place = lax.axis_index("row") * lax.axis_size("col") + lax.axis_index("col")
    spots = place.astype(jnp.int32).reshape(1)
    flow_room = scratch(3, 2 * PAD + codes[0].shape[0], LANES)
    on_pairs = lambda i: (i, i ^ 1)
    off_pairs = lambda i: (i, i + 1 if i % 2 else i - 1)

    def relay_off_pairs():
        count = lax.axis_size("col")
        pairs = [off_pairs(i) for i in range(count)]
        return [
            (r * count + i, (r ^ 1) * count + j)
            for r in range(lax.axis_size("row"))
            for i, j in pairs
            if 0 <= j < count
        ]

    def cut(source, pieces, shapes, space):
        return pl.pallas_call(
            functools.partial(cut_kernel, pieces),
            in_specs=[SCALARS, pl.BlockSpec(memory_space=space)],
            out_specs=[HERE] * len(pieces),
            out_shape=[shape(*dims) for dims in shapes],
            scratch_shapes=[pltpu.SemaphoreType.DMA((len(pieces),))],
            cost_estimate=cost(0, 1 << 22),
            compiler_params=ROOM,
        )(spots, source)

    chunks = range(0, cols, LANES)
    late = chunks[-1]
    hbm = pltpu.HBM
    far_field = pltpu.with_memory_space_constraint(covariance, hbm)
    (raw_0,) = cut(far_field, [(0, 0)], [(rows, LANES)], hbm)
    raw_late, edge = cut(covariance, [(0, late), ("outer", 0)], [(rows, LANES), (HALO, late)], hbm)
    swap = lambda piece: shifted(piece, "row", lambda i: (i, i ^ 1))
    x_out = lambda i: (i, i + 2 if i % 2 else i - 2)
    x_in = lambda i: (i, i - 2 if i % 2 else i + 2)
    swapped = [swap(raw_0)]
    crossed = lax.ppermute(raw_late, ("row", "col"), relay_off_pairs())
    far_other = shifted(edge, "row", x_out)
    raw_1, above, below = cut(
        covariance, [(0, LANES), (rows - HALO, late), (0, late)], [(rows, LANES), (HALO, LANES), (HALO, LANES)], hbm
    )
    swapped.append(swap(raw_1))
    above = shifted(above, "row", lambda i: (i, i + 1))
    below = shifted(below, "row", lambda i: (i, i - 1))
    near_field = near(covariance)
    spread = pl.pallas_call(
        adjoint_kernel,
        in_specs=[SCALARS, HERE, HERE, HERE],
        out_specs=[HERE, HERE],
        out_shape=[jax.ShapeDtypeStruct((3 * HALO, cols), jnp.bfloat16)] * 2,
        scratch_shapes=[
            flow_room,
            scratch(KINDS, 3 * HALO + 2 * GY, LANES),
            scratch(3 * HALO + 2 * GY, cols),
            scratch(3 * HALO, cols),
        ],
        cost_estimate=cost(2 * 6 * 4 * 3 * HALO * cols, 4 * 3 * HALO * cols),
        compiler_params=ROOM,
        name="spread",
    )(spots, *codes)
    spread = [near(part) for part in spread]
    long = rows + 2 * HALO
    wide = pl.pallas_call(
        functools.partial(weights_kernel, lines),
        in_specs=[SCALARS] + [HERE] * 3,
        out_specs=HERE,
        out_shape=shape(KINDS, rows + long, LANES),
        scratch_shapes=[flow_room],
        cost_estimate=cost(0, 1 << 24),
        compiler_params=WIDE_ROOM,
        name="weights",
    )(spots, *codes)

    def block_part(mode, lane, far, field, other):
        outs = [shape(rows, LANES)] + ([shape(HALO, LANES)] if mode == "passed" else [])
        return pl.pallas_call(
            functools.partial(block_kernel, mode, lane),
            in_specs=[SCALARS] + [HERE] * 4,
            out_specs=[HERE] * len(outs),
            out_shape=outs,
            scratch_shapes=[scratch(long, LANES)] * 3,
            cost_estimate=cost(6 * 4 * rows * cols, 4 * rows * cols),
            compiler_params=ROOM,
        )(spots, near(wide), near(far), near(field), near(other))

    def call(terms, base, final=False):
        width = LANES * len(terms)
        moved = 4 * rows * (width + 2 * cols)
        return pl.pallas_call(
            functools.partial(product_kernel, [(kind, lane) for _, kind, lane in terms]),
            grid=(rows // SUB,),
            in_specs=[SCALARS] + [HERE] * (len(terms) + 3),
            out_specs=pl.BlockSpec((SUB, cols), lambda i: (i, 0)) if final else HERE,
            out_shape=shape(rows, cols),
            scratch_shapes=[pltpu.VMEM((3 * width, cols), jnp.bfloat16)],
            cost_estimate=cost(6 * rows * cols * width, moved),
            compiler_params=ROOM,
        )(spots, *[near(field) for field, _, _ in terms], *spread, near(base))

    kept, kept_on, relayed = [], [], []
    for number, other in enumerate(swapped):
        lane = chunks[number]
        passed, back = block_part("passed", lane, far_other, near_field, other)
        relayed.append(lax.ppermute(passed, ("row", "col"), relay_off_pairs()))
        far_mine = shifted(back, "row", x_in)
        kept += block_part("kept", lane, far_mine, near_field, other)
        kept_on.append(shifted(kept[-1], "col", on_pairs))
    turned = swap(crossed)
    (crossed_edge,) = cut(crossed, [("inner", 0)], [(HALO, LANES)], pl.ANY)
    far_off = shifted(crossed_edge, "row", x_in)
    kept += block_part("own", late, above, near_field, below)
    kept_on.append(shifted(kept[-1], "col", on_pairs))
    relayed += block_part("off", 0, far_off, turned, crossed)

    def near_terms(number):
        lane = chunks[number]
        return [(kept[number], "own", lane), (kept_on[number], "on", lane)]

    def far_terms(number):
        return [(relayed[number], "off", chunks[number])]

    result = call(near_terms(0), process_noise)
    result = call(near_terms(1) + far_terms(0), result)
    return call(near_terms(2) + far_terms(1) + far_terms(2), result, True)


def solution(mesh):
    return jax.shard_map(
        body,
        mesh=mesh,
        in_specs=(P("row", "col"), P("row", "col"), P(), P(), P()),
        out_specs=P("row", "col"),
        check_vma=False,
    )
```
